32 devices in a mesh: dp: 8 (over z, x), tensor: 4 (over y, core).
Axes of the slice: x: 2, y: 2, z: 4, core: 2. Of those that a mesh axis runs over, the one named last changes fastest.
Arguments:
- residual_in: float32 [8, 1024, 640], P('dp', 'tensor'), may hold values from -6 to 6
- positions: int32 [8, 1024], P('dp'), may hold values from 0 to 2047
- segments: int32 [8, 1024], P('dp'), may hold values from 0 to 7, never falling along the last dimension, each value on 1 to 512 neighbouring positions
- gain_in: float32 [640], replicated, may hold values from 0.5 to 1.5
- w_query: bfloat16 [640, 1024], P(None, 'tensor'), may hold values from -1 to 1
- w_key: bfloat16 [640, 256], replicated, may hold values from -1 to 1
- w_value: bfloat16 [640, 256], replicated, may hold values from -0.25 to 0.25
- gain_query: float32 [256], replicated, may hold values from 0.5 to 4
- gain_key: float32 [256], replicated, may hold values from 0.5 to 4
- w_out: bfloat16 [1024, 640], P('tensor'), may hold values from -0.1875 to 0.1875
- gain_attn: float32 [640], replicated, may hold values from 0.5 to 1.5
- gain_pre: float32 [640], replicated, may hold values from 0.5 to 1.5
- w_gate: bfloat16 [640, 2048], P(None, 'tensor'), may hold values from -0.25 to 0.25
- w_up: bfloat16 [640, 2048], P(None, 'tensor'), may hold values from -0.25 to 0.25
- w_down: bfloat16 [2048, 640], P('tensor'), may hold values from -0.125 to 0.125
- gain_post: float32 [640], replicated, may hold values from 0.5 to 1.5
- cotangent: float32 [8, 1024, 640], P('dp', 'tensor'), may hold values from -6 to 6
Outputs:
- layer_out: float32 [8, 1024, 640], P('dp', 'tensor')
- grad_input: float32 [8, 1024, 640], P('dp', 'tensor')
- grad_gain_in: float32 [640], replicated
- grad_w_query: float32 [640, 1024], P(None, 'tensor')
- grad_w_key: float32 [640, 256], replicated
- grad_w_value: float32 [640, 256], replicated
- grad_gain_query: float32 [256], replicated
- grad_gain_key: float32 [256], replicated
- grad_w_out: float32 [1024, 640], P('tensor')
- grad_gain_attn: float32 [640], replicated
- grad_gain_pre: float32 [640], replicated
- grad_w_gate: float32 [640, 2048], P(None, 'tensor')
- grad_w_up: float32 [640, 2048], P(None, 'tensor')
- grad_w_down: float32 [2048, 640], P('tensor')
- grad_gain_post: float32 [640], replicated
The draws below stay inside these ranges and needn't reach their ends.
Inputs may be any that keep to these rules, and one draw needn't show every extreme that they name: `segments`: ids never fall along a packed row, each document holds 1 to 512 tokens, and every row has one document of exactly 512 tokens.
All inputs are finite; a program needn't handle non-finite values.
Results may differ from the reference program's by a relative error of at most 0.02.
The reference program's roundings to bfloat16 on the way count: a program that leaves them out, or rounds other values in their place, can miss the bound.
Values may be sent and summed in bfloat16 or wider, within the bound.
No kernel may reach another device: no remote copies, remote signals or barrier semaphores. Data moves between devices by JAX's collectives and lax.ppermute only.
A program may use at most 128 MiB of HBM per device.

```python
import math
import jax
import jax.numpy as jnp
import numpy as np
from jax import lax

D = 640
HEADS = 4
HD = 256
FF = 2048
WINDOW = 512
TOK_DEV = 1024
ROWS = 8


def pair_weights(key):
    first, second = jax.random.split(jax.random.fold_in(key, 17))
    scale_factor = D ** (-0.5)
    query_part = jax.random.truncated_normal(first, -4.0, 4.0, (D, HEADS * HD), jnp.float32) * scale_factor
    fresh_part = jax.random.truncated_normal(second, -4.0, 4.0, (D, HD), jnp.float32) * scale_factor
    key_part = fresh_part
    return (query_part, key_part)


def draw_w_query(key, part):
    return pair_weights(key)[0].astype(jnp.bfloat16)


def draw_w_key(key, part):
    return pair_weights(key)[1].astype(jnp.bfloat16)


def gain_values(key, salt):
    unit = jax.random.uniform(jax.random.fold_in(key, salt), (HD,), jnp.float32)
    return jnp.exp(math.log(0.7) + unit * math.log(2.0))


def draw_gain_query(key, part):
    return gain_values(key, 23)


def draw_gain_key(key, part):
    return gain_values(key, 29)


def touch_ends(values, stream_key, low, top_value):
    index_at = [jax.random.randint(jax.random.fold_in(stream_key, axis), (), 0, length) for axis, length in enumerate(values.shape)]
    longest = values.shape.index(max(values.shape))
    beside = index_at[:longest] + [(index_at[longest] + 1) % values.shape[longest]] + index_at[longest + 1:]
    return values.at[tuple(index_at)].set(low).at[tuple(beside)].set(top_value)


def level_of(rng, extent, cuts, smallest, largest):
    loudness, own = 1.0, jax.random.fold_in(rng, 6)
    for position, shards_of in cuts:
        heights = jnp.exp(jax.random.uniform(jax.random.fold_in(own, position), (shards_of,), jnp.float32, smallest / len(cuts), largest / len(cuts)))
        loudness = loudness * jnp.repeat(heights, extent[position] // shards_of).reshape([-1 if axis == position else 1 for axis in range(len(extent))])
    return loudness


def profile(number_of, total, limit, lean):
    portions = [(1 << 20) // math.isqrt(standing ** lean) + 1 for standing in range(2, number_of + 1)]
    surplus, counts = total - limit - (number_of - 1), [1] * (number_of - 1)
    while surplus > 0:
        free = [i for i in range(number_of - 1) if counts[i] < limit]
        mass, remaining = sum([portions[i] for i in free]), surplus
        for i in free:
            more = min(limit - counts[i], max(1, remaining * portions[i] // mass), surplus)
            counts[i] = counts[i] + more
            surplus = surplus - more
    return np.array([limit] + counts)


def uneven_parts(key, count, total, reach, lean):
    if count == 2:
        one = jax.random.randint(key, (), max(1, total - reach), min(reach, total - 1) + 1)
        return jnp.stack([one, total - one])
    tallies = jnp.asarray(profile(count, total, reach, lean), jnp.int32)
    couples = (count - 1) // 2
    donor, receiver = tallies[1:1 + 2 * couples:2], tallies[2:2 + 2 * couples:2]
    room = jnp.minimum(donor - 1, reach - receiver)
    passed = jax.random.randint(jax.random.fold_in(key, 1), (couples,), 0, 1 << 20) % (room + 1)
    tallies = tallies.at[1:1 + 2 * couples:2].set(donor - passed).at[2:2 + 2 * couples:2].set(receiver + passed)
    return tallies[jax.random.permutation(jax.random.fold_in(key, 2), count)]


def centred(own_key, shape, scale, limit, cuts=(), kind=jnp.bfloat16):
    level = level_of(own_key, shape, cuts, -0.22, 0.18) if cuts else 1.0
    result = jax.random.normal(own_key, shape, jnp.float32) * scale * level
    return jnp.minimum(jnp.maximum(result, -limit), limit).astype(kind)


def setup_inputs(seed: int = 0) -> dict:
    streams_of = jax.random.split(jax.random.key(seed), 18)
    residual_in = centred(streams_of[0], (ROWS, TOK_DEV, D), 1.0, 6.0, ((0, 8), (1, 4)), jnp.float32)
    positions = touch_ends(jax.random.randint(streams_of[1], (ROWS, TOK_DEV), 0, 2048), jax.random.fold_in(streams_of[1], 1), 0, 2047).astype(jnp.int32)
    segments = jax.vmap(lambda own: jnp.searchsorted(jnp.cumsum(uneven_parts(own, TOK_DEV // (WINDOW // 4), TOK_DEV, WINDOW, 2)), jnp.arange(TOK_DEV), side="right"))(jax.random.split(streams_of[2], ROWS)).reshape((ROWS, TOK_DEV)).astype(jnp.int32)
    gain_in = jnp.clip(1.0 + 0.1 * jax.random.normal(streams_of[3], (D,), jnp.float32), 0.5, 1.5)
    w_query = draw_w_query(jax.random.fold_in(streams_of[17], 71), 0)
    w_key = draw_w_key(jax.random.fold_in(streams_of[17], 71), 0)
    w_value = centred(streams_of[6], (D, HD), D ** -0.5, 0.25)
    gain_query = draw_gain_query(jax.random.fold_in(streams_of[17], 71), 0)
    gain_key = draw_gain_key(jax.random.fold_in(streams_of[17], 71), 0)
    w_out = centred(streams_of[9], (HEADS * HD, D), (HEADS * HD) ** -0.5, 0.1875, ((0, 4),))
    gain_attn = jnp.clip(1.0 + 0.1 * jax.random.normal(streams_of[10], (D,), jnp.float32), 0.5, 1.5)
    gain_pre = jnp.clip(1.0 + 0.1 * jax.random.normal(streams_of[11], (D,), jnp.float32), 0.5, 1.5)
    w_gate = centred(streams_of[12], (D, FF), D ** -0.5, 0.25, ((1, 4),))
    w_up = centred(streams_of[13], (D, FF), D ** -0.5, 0.25, ((1, 4),))
    w_down = centred(streams_of[14], (FF, D), FF ** -0.5, 0.125, ((0, 4),))
    gain_post = jnp.clip(1.0 + 0.1 * jax.random.normal(streams_of[15], (D,), jnp.float32), 0.5, 1.5)
    cotangent = centred(streams_of[16], (ROWS, TOK_DEV, D), 1.0, 6.0, ((0, 8), (1, 4)), jnp.float32)
    return dict(residual_in=residual_in, positions=positions, segments=segments, gain_in=gain_in, w_query=w_query, w_key=w_key, w_value=w_value, gain_query=gain_query, gain_key=gain_key, w_out=w_out, gain_attn=gain_attn, gain_pre=gain_pre, w_gate=w_gate, w_up=w_up, w_down=w_down, gain_post=gain_post, cotangent=cotangent)


EPSILON = 1e-06

def rms_forward(values, gain):
    factor = lax.rsqrt(lax.optimization_barrier(jnp.mean(values * values, axis=-1, keepdims=True)) + EPSILON)
    return (values * factor * gain, factor)

def rms_backward(values, factor, gain, upstream):
    unit_vals = values * factor
    weighted = upstream * gain
    inner = lax.optimization_barrier(jnp.mean(weighted * unit_vals, axis=-1, keepdims=True))
    back = factor * (weighted - unit_vals * inner)
    gain_grad = lax.optimization_barrier(jnp.sum((upstream * unit_vals).reshape(-1, values.shape[-1]), axis=0))
    return (back, gain_grad)

def rope_tables(spots, width):
    half_width = width // 2
    inverse = jnp.exp(jnp.arange(half_width, dtype=jnp.float32) * (-2.0 * math.log(10000.0) / width))
    angles = spots.astype(jnp.float32)[:, None] * inverse[None, :]
    return (jnp.cos(angles), jnp.sin(angles))

def rotate(values, cosine, sine_part):
    half_width = values.shape[-1] // 2
    first = values[..., :half_width]
    second = values[..., half_width:]
    return jnp.concatenate([first * cosine - second * sine_part, second * cosine + first * sine_part], axis=-1)

def gelu_parts(values):
    coeff = math.sqrt(2.0 / math.pi)
    tangent = jnp.tanh(coeff * (values + 0.044715 * values * values * values))
    output = 0.5 * values * (1.0 + tangent)
    slope = 0.5 * (1.0 + tangent) + 0.5 * values * (1.0 - tangent * tangent) * coeff * (1.0 + 3.0 * 0.044715 * values * values)
    return (output, slope)

def key_windows(values, filler):
    lead = jnp.full((WINDOW,) + values.shape[1:], filler, values.dtype)
    padded = jnp.concatenate([lead, values], axis=0)
    blocks = values.shape[0] // WINDOW
    block_shape = (blocks, WINDOW) + values.shape[1:]
    return jnp.concatenate([padded[:-WINDOW].reshape(block_shape), values.reshape(block_shape)], axis=1)

def allowed_mask(docs_query, docs_key):
    row_index = lax.broadcasted_iota(jnp.int32, (WINDOW, 2 * WINDOW), 0)
    col_index = lax.broadcasted_iota(jnp.int32, (WINDOW, 2 * WINDOW), 1)
    same_doc = docs_query[:, None] == docs_key[None, :]
    return same_doc & (col_index > row_index) & (col_index <= row_index + WINDOW)

def block_scores(query_blk, key_blk, docs_query, docs_key):
    raw_scores = jnp.einsum('qhd,kd->hqk', query_blk.astype(jnp.float32), key_blk.astype(jnp.float32)) / math.sqrt(HD)
    return jnp.where(allowed_mask(docs_query, docs_key)[None], raw_scores, -1e+30)

def attend_block(operands):
    query_blk, key_blk, value_blk, docs_query, docs_key = operands
    scores = block_scores(query_blk, key_blk, docs_query, docs_key)
    highest = lax.optimization_barrier(jnp.max(scores, axis=-1, keepdims=True))
    log_total = highest + jnp.log(lax.optimization_barrier(jnp.sum(jnp.exp(scores - highest), axis=-1, keepdims=True)))
    probs = jnp.exp(scores - log_total).astype(jnp.bfloat16)
    attended = jnp.einsum('hqk,kd->qhd', probs.astype(jnp.float32), value_blk.astype(jnp.float32)).astype(jnp.bfloat16)
    return (attended, log_total[..., 0])

def attend_back(operands):
    query_blk, key_blk, value_blk, docs_query, docs_key, log_total, upstream = operands
    scores = block_scores(query_blk, key_blk, docs_query, docs_key)
    probs = jnp.exp(scores - log_total[..., None])
    probs_low = probs.astype(jnp.bfloat16)
    dprob = jnp.einsum('qhd,kd->hqk', upstream.astype(jnp.float32), value_blk.astype(jnp.float32))
    delta = lax.optimization_barrier(jnp.sum(probs * dprob, axis=-1, keepdims=True))
    dscore = (probs * (dprob - delta) / math.sqrt(HD)).astype(jnp.bfloat16)
    grad_query = jnp.einsum('hqk,kd->qhd', dscore.astype(jnp.float32), key_blk.astype(jnp.float32))
    grad_key = jnp.einsum('hqk,qhd->khd', dscore.astype(jnp.float32), query_blk.astype(jnp.float32))
    grad_value = jnp.einsum('hqk,qhd->khd', probs_low.astype(jnp.float32), upstream.astype(jnp.float32))
    return (grad_query, grad_key, grad_value)

def spread_keys(parts):
    early = parts[:, :WINDOW]
    late = parts[:, WINDOW:]
    moved = jnp.concatenate([early[1:], jnp.zeros_like(early[:1])], axis=0)
    return (late + moved).reshape((-1,) + parts.shape[2:])

def attention_forward(query_rot, key_rot, value_low, docs):
    blocks = query_rot.shape[0] // WINDOW
    operands = (query_rot.reshape((blocks, WINDOW) + query_rot.shape[1:]), key_windows(key_rot, 0), key_windows(value_low, 0), docs.reshape(blocks, WINDOW), key_windows(docs, -1))
    attended, log_total = lax.map(attend_block, operands)
    return (attended.reshape(query_rot.shape), log_total, operands)

def attention_backward(operands, log_total, upstream):
    blocks = upstream.shape[0] // WINDOW
    upstream_blocks = upstream.reshape((blocks, WINDOW) + upstream.shape[1:])
    grad_query, grad_key, grad_value = lax.map(attend_back, operands + (log_total, upstream_blocks))
    return (grad_query.reshape(upstream.shape), spread_keys(grad_key), spread_keys(grad_value))

def add_pair(running, extra):
    return running + extra

def reference(residual_in, positions, segments, gain_in, w_query, w_key, w_value, gain_query, gain_key, w_out, gain_attn, gain_pre, w_gate, w_up, w_down, gain_post, cotangent):

    def per_row(carry, row_inputs):
        residual_row, spots, docs, upstream = row_inputs
        total = residual_row.shape[0]
        normed, factor_in = rms_forward(residual_row, gain_in)
        normed_low = normed.astype(jnp.bfloat16)
        query = jnp.dot(normed_low, w_query, preferred_element_type=jnp.float32).reshape(total, HEADS, HD)
        keyed = jnp.dot(normed_low, w_key, preferred_element_type=jnp.float32)
        valued = jnp.dot(normed_low, w_value, preferred_element_type=jnp.float32)
        query_normed, factor_query = rms_forward(query, gain_query)
        key_normed, factor_key = rms_forward(keyed, gain_key)
        cosine, sine_part = rope_tables(spots, HD)
        query_rot = rotate(query_normed, cosine[:, None], sine_part[:, None]).astype(jnp.bfloat16)
        key_rot = rotate(key_normed, cosine, sine_part).astype(jnp.bfloat16)
        value_low = valued.astype(jnp.bfloat16)
        attended, log_total, operands = attention_forward(query_rot, key_rot, value_low, docs)
        flat = attended.reshape(total, HEADS * HD)
        branch = jnp.dot(flat, w_out, preferred_element_type=jnp.float32)
        post_attn, factor_attn = rms_forward(branch, gain_attn)
        middle = residual_row + post_attn
        normed_two, factor_pre = rms_forward(middle, gain_pre)
        normed_two_low = normed_two.astype(jnp.bfloat16)
        gate = jnp.dot(normed_two_low, w_gate, preferred_element_type=jnp.float32)
        up_proj = jnp.dot(normed_two_low, w_up, preferred_element_type=jnp.float32)
        activated, slope = gelu_parts(gate)
        hidden = (activated * up_proj).astype(jnp.bfloat16)
        ffn_out = jnp.dot(hidden, w_down, preferred_element_type=jnp.float32)
        post_ffn, factor_post = rms_forward(ffn_out, gain_post)
        result_row = middle + post_ffn
        grad_ffn, grad_gain_post = rms_backward(ffn_out, factor_post, gain_post, upstream)
        grad_ffn_low = grad_ffn.astype(jnp.bfloat16)
        grad_w_down = jnp.dot(hidden.T, grad_ffn_low, preferred_element_type=jnp.float32)
        grad_hidden = jnp.dot(grad_ffn_low, w_down.T, preferred_element_type=jnp.float32)
        grad_up = (grad_hidden * activated).astype(jnp.bfloat16)
        grad_gate = (grad_hidden * up_proj * slope).astype(jnp.bfloat16)
        grad_w_gate = jnp.dot(normed_two_low.T, grad_gate, preferred_element_type=jnp.float32)
        grad_w_up = jnp.dot(normed_two_low.T, grad_up, preferred_element_type=jnp.float32)
        grad_normed_two = jnp.dot(grad_gate, w_gate.T, preferred_element_type=jnp.float32) + jnp.dot(grad_up, w_up.T, preferred_element_type=jnp.float32)
        back_pre, grad_gain_pre = rms_backward(middle, factor_pre, gain_pre, grad_normed_two)
        grad_middle = upstream + back_pre
        grad_branch, grad_gain_attn = rms_backward(branch, factor_attn, gain_attn, grad_middle)
        grad_branch_low = grad_branch.astype(jnp.bfloat16)
        grad_w_out = jnp.dot(flat.T, grad_branch_low, preferred_element_type=jnp.float32)
        grad_attended = jnp.dot(grad_branch_low, w_out.T, preferred_element_type=jnp.float32).astype(jnp.bfloat16).reshape(total, HEADS, HD)
        grad_query_rot, grad_key_rot, grad_value = attention_backward(operands, log_total, grad_attended)
        grad_query, grad_gain_query = rms_backward(query, factor_query, gain_query, rotate(grad_query_rot, cosine[:, None], -sine_part[:, None]))
        grad_key, grad_gain_key = rms_backward(keyed[:, None], factor_key[:, None], gain_key, rotate(grad_key_rot, cosine[:, None], -sine_part[:, None]))
        query_low = grad_query.reshape(total, HEADS * HD).astype(jnp.bfloat16)
        key_low = grad_key.astype(jnp.bfloat16)
        value_grad_low = grad_value.astype(jnp.bfloat16)
        normed_wide = normed_low.astype(jnp.float32)
        grad_w_query = jnp.dot(normed_low.T, query_low, preferred_element_type=jnp.float32)
        grad_w_key = jnp.einsum('td,thk->dk', normed_wide, key_low.astype(jnp.float32))
        grad_w_value = jnp.einsum('td,thk->dk', normed_wide, value_grad_low.astype(jnp.float32))
        grad_normed = jnp.dot(query_low, w_query.T, preferred_element_type=jnp.float32) + jnp.einsum('thk,dk->td', key_low.astype(jnp.float32), w_key.astype(jnp.float32)) + jnp.einsum('thk,dk->td', value_grad_low.astype(jnp.float32), w_value.astype(jnp.float32))
        back_in, grad_gain_in = rms_backward(residual_row, factor_in, gain_in, grad_normed)
        grad_row = grad_middle + back_in
        grads = (grad_gain_in, grad_w_query, grad_w_key, grad_w_value, grad_gain_query, grad_gain_key, grad_w_out, grad_gain_attn, grad_gain_pre, grad_w_gate, grad_w_up, grad_w_down, grad_gain_post)
        return (jax.tree.map(add_pair, carry, grads), (result_row, grad_row))
    initial = (jnp.zeros((D,), jnp.float32), jnp.zeros((D, HEADS * HD), jnp.float32), jnp.zeros((D, HD), jnp.float32), jnp.zeros((D, HD), jnp.float32), jnp.zeros((HD,), jnp.float32), jnp.zeros((HD,), jnp.float32), jnp.zeros((HEADS * HD, D), jnp.float32), jnp.zeros((D,), jnp.float32), jnp.zeros((D,), jnp.float32), jnp.zeros((D, FF), jnp.float32), jnp.zeros((D, FF), jnp.float32), jnp.zeros((FF, D), jnp.float32), jnp.zeros((D,), jnp.float32))
    totals, (outputs, grad_inputs) = lax.scan(per_row, initial, (residual_in, positions, segments, cotangent))
    return (outputs, grad_inputs, totals[0], totals[1], totals[2], totals[3], totals[4], totals[5], totals[6], totals[7], totals[8], totals[9], totals[10], totals[11], totals[12])
```

```python
import math

import jax
import jax.numpy as jnp
from jax import lax
from jax.sharding import PartitionSpec as P

WINDOW = 512

EPSILON = 1e-06

LOW = jnp.bfloat16
WIDE = jnp.float32


def rms_forward(values, gain):
    factor = lax.rsqrt(jnp.mean(values * values, axis=-1, keepdims=True) + EPSILON)
    return (values * factor * gain, factor)


def rms_backward(values, factor, gain, upstream):
    unit_vals = values * factor
    weighted = upstream * gain
    inner = jnp.mean(weighted * unit_vals, axis=-1, keepdims=True)
    back = factor * (weighted - unit_vals * inner)
    gain_grad = jnp.sum((upstream * unit_vals).reshape(-1, values.shape[-1]), axis=0)
    return (back, gain_grad)


def rope_tables(spots, width):
    half_width = width // 2
    inverse = jnp.exp(
        jnp.arange(half_width, dtype=jnp.float32) * (-2.0 * math.log(10000.0) / width)
    )
    angles = spots.astype(jnp.float32)[:, None] * inverse[None, :]
    return (jnp.cos(angles), jnp.sin(angles))


def rotate(values, cosine, sine_part):
    half_width = values.shape[-1] // 2
    first = values[..., :half_width]
    second = values[..., half_width:]
    return jnp.concatenate(
        [first * cosine - second * sine_part, second * cosine + first * sine_part], axis=-1
    )


def gelu_parts(values):
    coeff = math.sqrt(2.0 / math.pi)
    tangent = jnp.tanh(coeff * (values + 0.044715 * values * values * values))
    output = 0.5 * values * (1.0 + tangent)
    slope = 0.5 * (1.0 + tangent) + 0.5 * values * (1.0 - tangent * tangent) * coeff * (
        1.0 + 3.0 * 0.044715 * values * values
    )
    return (output, slope)


def mm(left, right):
    return jnp.dot(left, right, preferred_element_type=WIDE)


def mm_nt(left, right):
    return lax.dot_general(left, right, (((1,), (1,)), ((), ())), preferred_element_type=WIDE)


def mm_tn(left, right):
    return lax.dot_general(left, right, (((0,), (0,)), ((), ())), preferred_element_type=WIDE)


def swap(values, axis, size, bit):
    return lax.ppermute(values, axis, [(i, i ^ bit) for i in range(size)])


def add_low(mine, other):
    return (mine.astype(WIDE) + other.astype(WIDE)).astype(LOW)


def bits_of(size):
    if size & (size - 1):
        raise ValueError("axis size")
    return [1 << i for i in range(size.bit_length() - 1)]


def halves(values, upper):
    rows = values.shape[0] // 2
    keep = lax.dynamic_slice_in_dim(values, upper * rows, rows, 0)
    send = lax.dynamic_slice_in_dim(values, (1 - upper) * rows, rows, 0)
    return keep, send


def scatter_sum(values, axis, size):
    place = lax.axis_index(axis)
    for bit in bits_of(size):
        upper = (place & bit) // bit
        keep, send = halves(values, upper)
        values = add_low(keep, swap(send, axis, size, bit))
    return values


def gather_back(values, axis, size):
    place = lax.axis_index(axis)
    for bit in reversed(bits_of(size)):
        upper = (place & bit) // bit
        other = swap(values, axis, size, bit)
        low_first = jnp.concatenate([values, other], axis=0)
        high_first = jnp.concatenate([other, values], axis=0)
        values = jnp.where(upper == 0, low_first, high_first)
    return values


def all_sum(values, axis, size):
    for bit in bits_of(size):
        values = values + swap(values, axis, size, bit)
    return values


def build(n_dp, n_tensor):
    near, far = 1, n_tensor // 2
    if n_tensor != 4:
        raise ValueError("tensor size")

    def beside(values):
        return swap(values, "tensor", n_tensor, near)

    def across(values):
        return swap(values, "tensor", n_tensor, far)

    def pair_sum(partial, wire):
        rows = partial.shape[0] // 2
        return partial[:rows] + beside(partial[rows:].astype(wire)).astype(WIDE)

    def pair_gather(mine):
        return jnp.concatenate([mine, beside(mine)], axis=0)

    def reduce_dp(values):
        return gather_back(scatter_sum(values, "dp", n_dp), "dp", n_dp)

    def on_device(
        residual_in,
        positions,
        segments,
        gain_in,
        w_query,
        w_key,
        w_value,
        gain_query,
        gain_key,
        w_out,
        gain_attn,
        gain_pre,
        w_gate,
        w_up,
        w_down,
        gain_post,
        cotangent,
    ):
        residual_rows = residual_in[0]
        upstream = cotangent[0]
        rows = residual_rows.shape[0]
        width = w_key.shape[1]
        me = lax.axis_index("tensor")
        order = [me, me ^ near, me ^ far, me ^ far ^ near]

        def block_of(table, which):
            return lax.dynamic_slice_in_dim(table, which * rows, rows, 0)

        w_query_far = across(w_query)
        w_out_far = across(w_out)
        w_gate_far = across(w_gate)
        w_up_far = across(w_up)
        w_down_far = across(w_down)

        spots = [block_of(positions[0], b) for b in order[:2]]
        docs = jnp.concatenate([block_of(segments[0], b) for b in order])
        token = jnp.concatenate([b * rows + jnp.arange(rows, dtype=jnp.int32) for b in order])
        cosine, sine_part = rope_tables(jnp.concatenate(spots), width)
        cos_own, sin_own = cosine[:rows], sine_part[:rows]

        normed, factor_in = rms_forward(residual_rows, gain_in)
        normed_low = normed.astype(LOW)
        keyed = mm(normed_low, w_key)
        valued = mm(normed_low, w_value)
        key_normed, factor_key = rms_forward(keyed, gain_key)
        key_rot = rotate(key_normed, cos_own, sin_own).astype(LOW)
        kv_own = jnp.concatenate([key_rot, valued.astype(LOW)], axis=1)
        kv_far = across(kv_own)
        kv_all = jnp.concatenate([kv_own, beside(kv_own), kv_far, beside(kv_far)], axis=0)
        key_all, value_all = kv_all[:, :width], kv_all[:, width:]

        chip_rows = pair_gather(normed_low)
        gap = token[: 2 * rows, None] - token[None, :]
        allowed = (docs[: 2 * rows, None] == docs[None, :]) & (gap >= 0) & (gap < WINDOW)

        scale = 1.0 / math.sqrt(width)
        saved = []
        partial = 0.0
        for w_q, w_o in ((w_query, w_out), (w_query_far, w_out_far)):
            query = mm(chip_rows, w_q)
            query_normed, factor_query = rms_forward(query, gain_query)
            query_rot = rotate(query_normed, cosine, sine_part).astype(LOW)
            scores = jnp.where(allowed, mm_nt(query_rot, key_all) * scale, -1e30)
            highest = jnp.max(scores, axis=-1, keepdims=True)
            log_total = highest + jnp.log(jnp.sum(jnp.exp(scores - highest), axis=-1, keepdims=True))
            probs = jnp.exp(scores - log_total).astype(LOW)
            attended = mm(probs, value_all).astype(LOW)
            saved.append((query, factor_query, query_rot, log_total, attended))
            partial = partial + mm(attended, w_o)
        branch = pair_sum(partial, WIDE)
        post_attn, factor_attn = rms_forward(branch, gain_attn)
        middle = residual_rows + post_attn
        normed_two, factor_pre = rms_forward(middle, gain_pre)
        chip_two = pair_gather(normed_two.astype(LOW))

        units = []
        partial = 0.0
        for w_g, w_u, w_d in ((w_gate, w_up, w_down), (w_gate_far, w_up_far, w_down_far)):
            gate = mm(chip_two, w_g)
            up_proj = mm(chip_two, w_u)
            activated, slope = gelu_parts(gate)
            hidden = (activated * up_proj).astype(LOW)
            units.append((activated, slope, up_proj, hidden))
            partial = partial + mm(hidden, w_d)
        ffn_out = pair_sum(partial, WIDE)
        post_ffn, factor_post = rms_forward(ffn_out, gain_post)
        result_rows = middle + post_ffn

        grad_ffn, grad_gain_post = rms_backward(ffn_out, factor_post, gain_post, upstream)
        chip_gf = pair_gather(grad_ffn.astype(LOW))
        back = []
        partial = 0.0
        for (w_g, w_u, w_d), (activated, slope, up_proj, hidden) in zip(
            ((w_gate_far, w_up_far, w_down_far), (w_gate, w_up, w_down)), units[::-1]
        ):
            grad_hidden = mm_nt(chip_gf, w_d)
            grad_up = (grad_hidden * activated).astype(LOW)
            grad_gate = (grad_hidden * up_proj * slope).astype(LOW)
            back.append((grad_up, grad_gate, hidden))
            partial = partial + mm_nt(grad_gate, w_g) + mm_nt(grad_up, w_u)
        (up_far, gate_far, hidden_far), (up_own, gate_own, hidden_own) = back
        down_in = across(mm_tn(hidden_far, chip_gf).astype(LOW))
        gate_in = across(mm_tn(chip_two, gate_far).astype(LOW))
        up_in = across(mm_tn(chip_two, up_far).astype(LOW))
        grad_w_down = (mm_tn(hidden_own, chip_gf) + down_in.astype(WIDE)).astype(LOW)
        grad_w_gate = (mm_tn(chip_two, gate_own) + gate_in.astype(WIDE)).astype(LOW)
        grad_w_up = (mm_tn(chip_two, up_own) + up_in.astype(WIDE)).astype(LOW)
        grad_w_down = reduce_dp(grad_w_down).astype(WIDE)
        grad_w_gate = reduce_dp(grad_w_gate).astype(WIDE)
        grad_w_up = reduce_dp(grad_w_up).astype(WIDE)

        grad_normed_two = pair_sum(partial, LOW)
        back_pre, grad_gain_pre = rms_backward(middle, factor_pre, gain_pre, grad_normed_two)
        grad_middle = upstream + back_pre
        grad_branch, grad_gain_attn = rms_backward(branch, factor_attn, gain_attn, grad_middle)
        chip_gb = pair_gather(grad_branch.astype(LOW))

        partial = 0.0
        grad_keys = 0.0
        grad_values = 0.0
        grad_gain_query = 0.0
        query_grads = []
        for (w_q, w_o), (query, factor_query, query_rot, log_total, attended) in zip(
            ((w_query_far, w_out_far), (w_query, w_out)), saved[::-1]
        ):
            grad_attended = mm_nt(chip_gb, w_o).astype(LOW)
            scores = jnp.where(allowed, mm_nt(query_rot, key_all) * scale, -1e30)
            probs = jnp.exp(scores - log_total)
            dprob = mm_nt(grad_attended, value_all)
            delta = jnp.sum(probs * dprob, axis=-1, keepdims=True)
            dscore = (probs * (dprob - delta) * scale).astype(LOW)
            grad_query_rot = mm(dscore, key_all)
            grad_keys = grad_keys + mm_tn(dscore, query_rot)
            grad_values = grad_values + mm_tn(probs.astype(LOW), grad_attended)
            grad_query, gain_part = rms_backward(
                query, factor_query, gain_query, rotate(grad_query_rot, cosine, -sine_part)
            )
            grad_gain_query = grad_gain_query + gain_part
            query_low = grad_query.astype(LOW)
            query_grads.append(query_low)
            partial = partial + mm_nt(query_low, w_q)
        out_in = across(mm_tn(saved[1][4], chip_gb).astype(LOW))
        grad_w_out = (mm_tn(saved[0][4], chip_gb) + out_in.astype(WIDE)).astype(LOW)
        grad_w_out = reduce_dp(grad_w_out).astype(WIDE)

        grad_kv = jnp.concatenate([grad_keys, grad_values], axis=1)
        mine = jnp.concatenate([grad_kv[:rows], grad_kv[2 * rows : 3 * rows]], axis=0)
        theirs = jnp.concatenate([grad_kv[rows : 2 * rows], grad_kv[3 * rows :]], axis=0)
        chip_kv = mine + beside(theirs.astype(LOW)).astype(WIDE)
        kv_total = chip_kv[:rows] + across(chip_kv[rows:].astype(LOW)).astype(WIDE)

        query_in = across(mm_tn(chip_rows, query_grads[0]).astype(LOW))
        grad_w_query = (mm_tn(chip_rows, query_grads[1]) + query_in.astype(WIDE)).astype(LOW)

        grad_key, grad_gain_key = rms_backward(
            keyed, factor_key, gain_key, rotate(kv_total[:, :width], cos_own, -sin_own)
        )
        key_low = grad_key.astype(LOW)
        value_low = kv_total[:, width:].astype(LOW)
        grad_normed = pair_sum(partial, LOW) + mm_nt(key_low, w_key) + mm_nt(value_low, w_value)
        back_in, grad_gain_in = rms_backward(residual_rows, factor_in, gain_in, grad_normed)
        grad_rows = grad_middle + back_in

        low_bit, high_bit = me & near, (me & far) // far
        both = jnp.stack([mm_tn(normed_low, key_low), mm_tn(normed_low, value_low)])
        kept = lax.dynamic_index_in_dim(both, low_bit, 0, False)
        sent = lax.dynamic_index_in_dim(both, 1 - low_bit, 0, False)
        one = kept + beside(sent.astype(LOW)).astype(WIDE)
        half = width // 2
        kept = lax.dynamic_slice_in_dim(one, high_bit * half, half, 1)
        sent = lax.dynamic_slice_in_dim(one, (1 - high_bit) * half, half, 1)
        quarter = (kept + across(sent.astype(LOW)).astype(WIDE)).astype(LOW)
        last = reduce_dp(jnp.concatenate([grad_w_query, quarter], axis=1))
        grad_w_query = last[:, : w_query.shape[1]].astype(WIDE)
        quarter = last[:, w_query.shape[1] :]
        other = across(quarter)
        one = jnp.where(
            high_bit == 0,
            jnp.concatenate([quarter, other], axis=1),
            jnp.concatenate([other, quarter], axis=1),
        )
        other = beside(one)
        grad_w_key = jnp.where(low_bit == 0, one, other).astype(WIDE)
        grad_w_value = jnp.where(low_bit == 0, other, one).astype(WIDE)

        gains = [
            grad_gain_in,
            grad_gain_attn,
            grad_gain_pre,
            grad_gain_post,
            grad_gain_query,
            grad_gain_key,
        ]
        packed = jnp.concatenate(gains).reshape(-1, 128)
        packed = all_sum(packed, "tensor", n_tensor)
        packed = all_sum(packed, "dp", n_dp).reshape(-1)
        summed = []
        start = 0
        for gain in gains:
            summed.append(packed[start : start + gain.shape[0]])
            start += gain.shape[0]
        grad_gain_in, grad_gain_attn, grad_gain_pre, grad_gain_post = summed[:4]
        grad_gain_query, grad_gain_key = summed[4:]
        return (
            result_rows[None],
            grad_rows[None],
            grad_gain_in,
            grad_w_query,
            grad_w_key,
            grad_w_value,
            grad_gain_query,
            grad_gain_key,
            grad_w_out,
            grad_gain_attn,
            grad_gain_pre,
            grad_w_gate,
            grad_w_up,
            grad_w_down,
            grad_gain_post,
        )

    return on_device


def solution(mesh):
    placed = (
        P("dp", "tensor", None),
        P("dp", None),
        P("dp", None),
        P(),
        P(None, "tensor"),
        P(),
        P(),
        P(),
        P(),
        P("tensor", None),
        P(),
        P(),
        P(None, "tensor"),
        P(None, "tensor"),
        P("tensor", None),
        P(),
        P("dp", "tensor", None),
    )
    return jax.shard_map(
        build(mesh.shape["dp"], mesh.shape["tensor"]),
        mesh=mesh,
        in_specs=placed,
        out_specs=(
            P("dp", "tensor", None),
            P("dp", "tensor", None),
            P(),
            P(None, "tensor"),
            P(),
            P(),
            P(),
            P(),
            P("tensor", None),
            P(),
            P(),
            P(None, "tensor"),
            P(None, "tensor"),
            P("tensor", None),
            P(),
        ),
        check_vma=False,
    )
```
